128 devices in a mesh: dp: 8 (over y_hi, x), seq: 16 (over y_lo, z, core).
Axes of the slice: x: 4, y: 4 (y_hi: 2, y_lo: 2; y = y_hi * 2 + y_lo), z: 4, core: 2. Of those that a mesh axis runs over, the one named last changes fastest.
Arguments:
- tokens: bfloat16 [8, 128, 128, 1024], P('dp', 'seq'), may hold values from -12 to 12
- lengths: int32 [8], P('dp'), may hold values from 8192 to 16384, as said below
- w_qkv: bfloat16 [3, 1024, 1024], replicated, may hold values from -0.1875 to 0.1875
- out_grad: bfloat16 [8, 128, 128, 1024], P('dp', 'seq'), may hold values from -6 to 6
Outputs:
- attention: bfloat16 [8, 128, 128, 1024], P('dp', 'seq')
- input_grad: bfloat16 [8, 128, 128, 1024], P('dp', 'seq')
- w_grads: float32 [3, 1024, 1024], P(None, 'seq', 'dp')
The draws below stay inside these ranges and needn't reach their ends.
Inputs may be any that keep to these rules, and one draw needn't show every extreme that they name: Samples at positions from lengths on are padding; some sequence is full and some has exactly 8192 valid samples.
All inputs are finite; a program needn't handle non-finite values.
Results may differ from the reference program's by a relative error of at most 0.04.
The reference program's roundings to bfloat16 on the way count: a program that leaves them out, or rounds other values in their place, can miss the bound.
Values may be sent and summed in bfloat16 or wider, within the bound.
A program may use at most 192 MiB of HBM per device.

```python
import math
import jax
import jax.numpy as jnp
from jax import lax

D = 1024
HEADS = 8
HEAD_DIM = 128
ROWS = 128
STRIDE = 128
SAMPLES = 16384
SEQS = 8


def draw_tokens(key, part):
    shape = (SEQS, ROWS, STRIDE, D)
    base_key = jax.random.fold_in(jax.random.fold_in(key, 11), 0)
    values = jnp.clip(jax.random.normal(base_key, shape, jnp.float32), -6.0, 6.0)
    return values.astype(jnp.bfloat16)


def draw_lengths(key, part):
    first_key, second_key = jax.random.split(jax.random.fold_in(key, 23), 2)
    values = jax.random.randint(first_key, (SEQS,), SAMPLES // 2, SAMPLES + 1)
    order = jax.random.permutation(second_key, SEQS)
    values = values.at[order[0]].set(SAMPLES).at[order[1]].set(SAMPLES // 2)
    return values.astype(jnp.int32)


def shard_levels(stream_key, dims, cuts, smallest, high):
    factor_of = 1.0
    for axis_at, blocks in cuts:
        steps = jax.random.uniform(jax.random.fold_in(jax.random.fold_in(stream_key, 6), axis_at), (blocks,), jnp.float32, smallest / len(cuts), high / len(cuts))
        factor_of = factor_of * jnp.repeat(jnp.exp(steps), dims[axis_at] // blocks).reshape((-1,) + (1,) * (len(dims) - 1 - axis_at))
    return factor_of


def normal_values(own_key, dims, spread, reach, shards=(), kind=jnp.bfloat16):
    result = jax.random.normal(own_key, dims, jnp.float32) * spread
    if len(shards) > 0:
        result = shard_levels(own_key, dims, shards, -0.22, 0.18) * result
    return jnp.clip(result, min=-reach, max=reach).astype(kind)


def setup_inputs(seed: int = 0) -> dict:
    seeds = jax.random.split(jax.random.key(seed), 5)
    tokens = draw_tokens(jax.random.fold_in(seeds[4], 71), 0)
    lengths = draw_lengths(jax.random.fold_in(seeds[4], 71), 0)
    w_qkv = normal_values(seeds[2], (3, D, D), D ** -0.5, 0.1875)
    out_grad = normal_values(seeds[3], (SEQS, ROWS, STRIDE, D), 1.0, 6.0, ((0, 8), (1, 16)))
    return dict(tokens=tokens, lengths=lengths, w_qkv=w_qkv, out_grad=out_grad)


SCORE_FORM = 'bqhe,bkhe->bqhk'
APPLY_FORM = 'bqhk,bkhe->bqhe'
BACK_FORM = 'bqhk,bqhe->bkhe'

def rounded(values):
    return lax.optimization_barrier(values.astype(jnp.bfloat16)).astype(jnp.float32)

def swap_axes(values):
    return jnp.swapaxes(values, 0, 1)

def part_forward(query_h, key_h, value_h, allowed):
    scaling = 1.0 / math.sqrt(query_h.shape[-1])
    scores = jnp.where(allowed, jnp.einsum(SCORE_FORM, query_h, key_h) * scaling, -1e+30)
    highest = lax.optimization_barrier(jnp.max(scores, axis=-1))
    weights = jnp.where(allowed, jnp.exp(scores - highest[..., None]), 0.0)
    totals = lax.optimization_barrier(jnp.sum(weights, axis=-1))
    mixed = jnp.einsum(APPLY_FORM, rounded(weights), value_h)
    return (highest, totals, mixed)

def part_back(query_h, key_h, value_h, grad_h, allowed, log_total, delta):
    scaling = 1.0 / math.sqrt(query_h.shape[-1])
    scores = jnp.where(allowed, jnp.einsum(SCORE_FORM, query_h, key_h) * scaling, -1e+30)
    weights = jnp.where(allowed, jnp.exp(scores - log_total[..., None]), 0.0)
    grad_weights = jnp.einsum(SCORE_FORM, grad_h, value_h)
    grad_scores = rounded(weights * (grad_weights - delta[..., None]))
    grad_value = rounded(jnp.einsum(BACK_FORM, rounded(weights), grad_h))
    grad_query = rounded(jnp.einsum(APPLY_FORM, grad_scores, key_h) * scaling)
    grad_key = rounded(jnp.einsum(BACK_FORM, grad_scores, query_h) * scaling)
    return (grad_query, grad_key, grad_value)

def one_sequence(tokens_s, length, grad_s, w_qkv):
    wide = w_qkv.astype(jnp.float32)
    inputs = tokens_s.astype(jnp.float32)
    stacked = rounded(jnp.einsum('rcd,jdf->jrcf', inputs, wide))
    shape_h = (ROWS, STRIDE, HEADS, HEAD_DIM)
    query_h = stacked[0].reshape(shape_h)
    key_h = stacked[1].reshape(shape_h)
    value_h = stacked[2].reshape(shape_h)
    col_ids = jnp.arange(STRIDE, dtype=jnp.int32)
    row_ids = jnp.arange(ROWS, dtype=jnp.int32)
    key_pos = row_ids[:, None, None] * STRIDE + col_ids[None, None, :]
    same_col = col_ids[None, None, :] == col_ids[None, :, None]
    row_allowed = (col_ids[None, None, :] <= col_ids[None, :, None]) & ((key_pos < length) | same_col)
    row_allowed = row_allowed[:, :, None, :]
    col_key_pos = row_ids[None, None, :] * STRIDE + col_ids[:, None, None]
    column_allowed = (row_ids[None, None, :] < row_ids[None, :, None]) & (col_key_pos < length)
    column_allowed = column_allowed[:, :, None, :]
    row_high, row_total, row_mixed = part_forward(query_h, key_h, value_h, row_allowed)
    col_high, col_total, col_mixed = part_forward(swap_axes(query_h), swap_axes(key_h), swap_axes(value_h), column_allowed)
    col_high = swap_axes(col_high)
    col_total = swap_axes(col_total)
    col_mixed = swap_axes(col_mixed)
    joint = jnp.maximum(row_high, col_high)
    row_factor = jnp.exp(row_high - joint)
    col_factor = jnp.exp(col_high - joint)
    joint_total = row_total * row_factor + col_total * col_factor
    log_total = joint + jnp.log(joint_total)
    combined = (row_mixed * row_factor[..., None] + col_mixed * col_factor[..., None]) / joint_total[..., None]
    attention = combined.reshape(ROWS, STRIDE, D).astype(jnp.bfloat16)
    attention_f = rounded(combined)
    grad_h = grad_s.astype(jnp.float32).reshape(shape_h)
    delta = lax.optimization_barrier(jnp.sum(attention_f * grad_h, axis=-1))
    row_grads = part_back(query_h, key_h, value_h, grad_h, row_allowed, log_total, delta)
    col_grads = part_back(swap_axes(query_h), swap_axes(key_h), swap_axes(value_h), swap_axes(grad_h), column_allowed, swap_axes(log_total), swap_axes(delta))
    row_parts = jnp.stack(row_grads).reshape(3, ROWS, STRIDE, D)
    col_parts = jnp.stack([swap_axes(item) for item in col_grads]).reshape(3, ROWS, STRIDE, D)
    input_grad = jnp.einsum('jrcf,jdf->rcd', row_parts, wide) + jnp.einsum('jrcf,jdf->rcd', col_parts, wide)
    weight_part = jnp.einsum('rcd,jrcf->jdf', inputs, row_parts) + jnp.einsum('rcd,jrcf->jdf', inputs, col_parts)
    return (attention, input_grad.astype(jnp.bfloat16), weight_part)

def reference(tokens, lengths, w_qkv, out_grad):

    def per_sequence(items):
        return one_sequence(items[0], items[1], items[2], w_qkv)
    attention, input_grad, weight_parts = lax.map(per_sequence, (tokens, lengths, out_grad))
    return (attention, input_grad, lax.optimization_barrier(jnp.sum(weight_parts, axis=0)))
```

```python
import math

import jax
import jax.numpy as jnp
from jax import lax
from jax.experimental import pallas as pl
from jax.experimental.pallas import tpu as pltpu
from jax.sharding import PartitionSpec as P

BF = jnp.bfloat16
F32 = jnp.float32
SCALE = 1.0 / math.sqrt(128.0)
HEADS = 8
NT_W = 512
MESH = pl.DeviceIdType.MESH


def nt(a, b):
    return lax.dot_general(a, b, (((1,), (1,)), ((), ())), preferred_element_type=F32)


def tn(a, b):
    return lax.dot_general(a, b, (((0,), (0,)), ((), ())), preferred_element_type=F32)


def nn(a, b):
    return jnp.dot(a, b, preferred_element_type=F32)


def cols(h):
    return slice(h * 128, h * 128 + 128)


def tile(t, width):
    return pl.ds(pl.multiple_of(t * width, width), width)


def allowed(side, index, length):
    key = lax.broadcasted_iota(jnp.int32, (128, 128), 0)
    query = lax.broadcasted_iota(jnp.int32, (128, 128), 1)
    if side == 0:
        return (key <= query) & ((index * 128 + key < length) | (key == query))
    return (key < query) & (key * 128 + index < length)


def pipelined(count, gap, first, second, third):
    for h in range(count + 2 * gap):
        if h < count:
            first(h)
        if 0 <= h - gap < count:
            second(h - gap)
        if 0 <= h - 2 * gap < count:
            third(h - 2 * gap)


def project(x_ref, w_ref, qkv, side, j):
    @pl.loop(0, 1024 // NT_W)
    def _(t):
        out = nn(x_ref[...].reshape(1024, 1024), w_ref[j, :, tile(t, NT_W)])
        qkv[j, side * 8 : side * 8 + 8, :, tile(t, NT_W)] = out.astype(BF).reshape(8, 128, NT_W)


def attend(qkv, g_ref, stats, side, me, length, store):
    @pl.loop(0, 8)
    def _(i):
        at = side * 8 + i
        mask = allowed(side, me * 8 + i, length)
        scores, weights = {}, {}

        def first(h):
            value = qkv[2, at, :, cols(h)]
            scores[h] = (nt(qkv[1, at, :, cols(h)], qkv[0, at, :, cols(h)]), nt(value, g_ref[i, :, cols(h)]))

        def second(h):
            score, grad = scores.pop(h)
            score = jnp.where(mask, score * SCALE, -1e30)
            highest = jnp.max(score, axis=0, keepdims=True)
            weight = jnp.exp(score - jnp.maximum(highest, -1e29))
            row = pl.ds(i * 8 + h, 1)
            stats[side, 0, row, :] = highest
            stats[side, 1, row, :] = jnp.sum(weight, axis=0, keepdims=True)
            stats[side, 2, row, :] = jnp.sum(weight * grad, axis=0, keepdims=True)
            weights[h] = weight.astype(BF)

        def third(h):
            store(i, h, tn(weights.pop(h), qkv[2, at, :, cols(h)]))

        pipelined(HEADS, 2, first, second, third)


def attend_back(qkv, g_ref, joint, side, me, length):
    @pl.loop(0, 8)
    def _(i):
        at = side * 8 + i
        mask = allowed(side, me * 8 + i, length)
        scores, probs = {}, {}

        def first(h):
            scores[h] = (
                nt(qkv[1, at, :, cols(h)], qkv[0, at, :, cols(h)]),
                nt(qkv[2, at, :, cols(h)], g_ref[i, :, cols(h)]),
            )

        def second(h):
            score, grad = scores.pop(h)
            row = pl.ds(i * 8 + h, 1)
            prob = jnp.where(mask, jnp.exp(score * SCALE - joint[side, 0, row, :]), 0.0)
            probs[h] = (prob.astype(BF), (prob * (grad - joint[side, 1, row, :])).astype(BF))

        def third(h):
            prob, grad_score = probs.pop(h)
            grad_value = nn(prob, g_ref[i, :, cols(h)])
            grad_key = nn(grad_score, qkv[0, at, :, cols(h)]) * SCALE
            grad_query = tn(grad_score, qkv[1, at, :, cols(h)]) * SCALE
            qkv[2, at, :, cols(h)] = grad_value.astype(BF)
            qkv[1, at, :, cols(h)] = grad_key.astype(BF)
            qkv[0, at, :, cols(h)] = grad_query.astype(BF)

        pipelined(HEADS, 2, first, second, third)


def regroup(raw, out):
    row = lax.broadcasted_iota(jnp.int32, (256, 256), 0)
    col = lax.broadcasted_iota(jnp.int32, (256, 256), 1)
    perm = ((row // 32 == col % 8) & ((row // 8) % 4 == col // 64) & (row % 8 == (col // 8) % 8)).astype(BF)

    @pl.loop(0, 4)
    def _(i):
        moved = nn(perm, raw[pl.ds(i * 4, 4)].reshape(256, 1024)).astype(BF)
        out[:, tile(i, 32), :] = moved.reshape(8, 32, 1024)


def transpose_into(x_ref, xt, side):
    @pl.loop(0, 8)
    def _(i):
        xt[:, pl.ds(pl.multiple_of(side * 1024 + i * 128, 128), 128)] = x_ref[i].T


def pack_stats(stats, sent, side):
    for s in range(3):
        sent[side, :, s] = stats[side, s].T.reshape(16, 8, 128)


def swap_groups(rows):
    parts = [rows[8 * o : 8 * o + 8, :] for o in range(8)]
    lane = lax.broadcasted_iota(jnp.int32, (8, 128), 1)
    for b in (1, 2, 4):
        high = (lane // b) % 2 == 1
        new = list(parts)
        for v in range(8):
            if v & b == 0:
                new[v] = jnp.where(high, pltpu.roll(parts[v | b], b, 1), parts[v])
                new[v | b] = jnp.where(high, parts[v | b], pltpu.roll(parts[v], 128 - b, 1))
        parts = new
    return jnp.concatenate(parts, axis=0)


def join_stats(stats, came, joint, side, coef=None):
    other = [swap_groups(came[side, :, s].reshape(128, 128).T[:64]) for s in range(3)]
    own = [stats[side, s, :64, :] for s in range(3)]
    top = jnp.maximum(own[0], other[0])
    own_factor = jnp.exp(own[0] - top)
    other_factor = jnp.exp(other[0] - top)
    total = own[1] * own_factor + other[1] * other_factor
    joint[side, 0] = top + jnp.log(total)
    joint[side, 1] = (own[2] * own_factor + other[2] * other_factor) / total
    if coef is not None:
        pair = jnp.concatenate([own_factor / total, other_factor / total], axis=0)
        coef[...] = pair.T


def make_kernel(dp_size, seq_size):
    def kernel(
        len_ref, tok3, tok4, g3, g4, w_hbm, att_o, dx_o, dw_o,
        x_v, g_v, w_v, raw_x, raw_g, xc, gc, qkv, mix_r, mix_c, mix_in, dxs, dx_in, xt,
        rsb, rc, r1, r2, r3, stats, sent, came, joint, coef,
        lsem, osem, own_sem, ss, rs, cs, cr, ts, tr,
    ):
        dp = lax.axis_index("dp")
        me = lax.axis_index("seq")
        core = me % 2
        z = (me // 2) % 4
        ylo = me // 8
        x = dp % 4
        yhi = dp // 4
        y = yhi * 2 + ylo
        length = len_ref[0]

        def along(axis, k):
            if axis == "x":
                c = (x + k) % 4
                return (yhi * 4 + c, me), c
            if axis == "y":
                c = (y + k) % 4
                return ((c // 2) * 4 + x, (c % 2) * 8 + z * 2 + core), c
            c = (z + k) % 4
            return (dp, ylo * 8 + c * 2 + core), c

        here = {"x": x, "y": y, "z": z}

        loads = [pltpu.make_async_copy(w_hbm.at[j], w_v.at[j], lsem.at[j]) for j in range(3)]
        loads.append(pltpu.make_async_copy(tok3, x_v, lsem.at[3]))
        loads.append(pltpu.make_async_copy(g3, g_v, lsem.at[4]))
        for at in (3, 0, 4, 1, 2):
            loads[at].start()

        barrier = pltpu.get_barrier_semaphore()

        @pl.loop(1, 16)
        def _(k):
            pl.semaphore_signal(barrier, inc=1, device_id=(dp, (me + k) % 16), device_id_type=MESH)

        for k in (1, 2, 3):
            pl.semaphore_signal(barrier, inc=1, device_id=along("x", k)[0], device_id_type=MESH)
        for c in (0, 1):
            pl.semaphore_signal(
                barrier, inc=1, device_id=((1 - yhi) * 4 + x, c * 8 + z * 2 + core), device_id_type=MESH
            )
        pl.semaphore_wait(barrier, 20)

        def exchange(n, src, dst):
            def remote(k):
                p = (me + k) % 16
                return pltpu.make_async_remote_copy(
                    src(p), dst(me), ss.at[n, k], rs.at[n, k], device_id=(dp, p), device_id_type=MESH
                )

            def local():
                return pltpu.make_async_copy(src(me), dst(me), own_sem.at[n])

            def start():
                @pl.loop(1, 16)
                def _(k):
                    remote(k).start()

                local().start()

            def arrived():
                @pl.loop(1, 16)
                def _(k):
                    back = (me + 16 - k) % 16
                    pltpu.make_async_remote_copy(
                        src(back), dst(back), ss.at[n, k], rs.at[n, k], device_id=(dp, back), device_id_type=MESH
                    ).wait_recv()

                local().wait()

            def sent_all():
                @pl.loop(1, 16)
                def _(k):
                    remote(k).wait_send()

            return start, arrived, sent_all

        half = lambda t: pl.ds(t * 512, 512)
        moves = [
            exchange(0, lambda p: tok4.at[:, p], lambda p: raw_x.at[p]),
            exchange(1, lambda p: g4.at[:, p], lambda p: raw_g.at[p]),
            exchange(2, lambda p: sent.at[0, p], lambda p: came.at[1, p]),
            exchange(3, lambda p: sent.at[1, p], lambda p: came.at[0, p]),
            exchange(4, lambda p: mix_c.at[:, p], lambda p: mix_in.at[p]),
            exchange(5, lambda p: dxs.at[:, p, :, half(0)], lambda p: dx_in.at[p, :, :, half(0)]),
            exchange(6, lambda p: dxs.at[:, p, :, half(1)], lambda p: dx_in.at[p, :, :, half(1)]),
        ]
        start = [m[0] for m in moves]
        arrived = [m[1] for m in moves]

        start[0]()
        start[1]()
        stats[...] = jnp.zeros_like(stats)

        loads[3].wait()
        for j in range(3):
            loads[j].wait()
            project(x_v, w_v, qkv, 0, j)
        loads[4].wait()

        def store_row(i, h, mixed):
            mix_r[i, :, cols(h)] = mixed.astype(BF)

        attend(qkv, g_v, stats, 0, me, length, store_row)
        pack_stats(stats, sent, 0)
        start[2]()

        arrived[0]()
        regroup(raw_x, xc)
        for j in range(3):
            project(xc, w_v, qkv, 1, j)
        transpose_into(x_v, xt, 0)
        transpose_into(xc, xt, 1)
        arrived[1]()
        regroup(raw_g, gc)

        def store_column(i, h, mixed):
            mix_c[i, :, :, cols(h)] = mixed.reshape(16, 8, 128).astype(BF)

        attend(qkv, gc, stats, 1, me, length, store_column)
        pack_stats(stats, sent, 1)
        start[3]()
        start[4]()

        arrived[2]()
        join_stats(stats, came, joint, 1)
        attend_back(qkv, gc, joint, 1, me, length)

        def input_tile(side, t):
            total = None
            for j in range(3):
                grads = qkv[j, side * 8 : side * 8 + 8].reshape(1024, 1024)
                term = nt(grads, w_v[j, tile(t, 512), :])
                total = term if total is None else total + term
            return total

        for t in range(2):
            dxs[:, :, :, t * 512 : t * 512 + 512] = input_tile(1, t).reshape(8, 16, 8, 512).astype(BF)
            start[5 + t]()

        arrived[3]()
        join_stats(stats, came, joint, 0, coef)
        attend_back(qkv, g_v, joint, 0, me, length)

        order = (("x", "y", "z"), ("y", "z", "x"), ("z", "x", "y"))

        def weight_grads(j):
            @pl.loop(0, 2)
            def _(t):
                out = nn(xt[...], qkv[j, :, :, tile(t, 512)].reshape(2048, 512)).astype(BF)
                for s in range(16):
                    for b in range(4):
                        pos = {"x": b, "y": t * 2 + s // 8, "z": (s // 2) % 4}
                        a1, a2, a3 = (pos[a] for a in order[j])
                        rsb[j, s % 2, a1 * 16 + a2 * 4 + a3] = out[s * 64 : s * 64 + 64, b * 128 : b * 128 + 128]

        def core_copy(j):
            return pltpu.make_async_remote_copy(
                rsb.at[j, 1 - core], rc.at[j], cs.at[j], cr.at[j], device_id=(dp, me + 1 - 2 * core), device_id_type=MESH
            )

        def stage_copies(j, stage):
            axis = order[j][stage]
            copies = []
            for k in (1, 2, 3):
                device, c = along(axis, k)
                if stage == 0:
                    src, dst = rsb.at[j, core, pl.ds(c * 16, 16)], r1.at[j, here[axis]]
                elif stage == 1:
                    src, dst = r1.at[j, here[order[j][0]], pl.ds(c * 4, 4)], r2.at[j, here[axis]]
                else:
                    src, dst = r2.at[j, here[order[j][1]], c], r3.at[j, here[axis]]
                n = j * 3 + stage
                copies.append(
                    pltpu.make_async_remote_copy(
                        src, dst, ts.at[n, k], tr.at[n, k], device_id=device, device_id_type=MESH
                    )
                )
            return copies

        def core_sum(j):
            core_copy(j).wait_recv()

            @pl.loop(0, 4)
            def _(t):
                at = pl.ds(t * 16, 16)
                rsb[j, core, at] = (rsb[j, core, at].astype(F32) + rc[j, at].astype(F32)).astype(BF)

        def stage_start(j, stage):
            for c in stage_copies(j, stage):
                c.start()

        def stage_sum(j, stage):
            for c in stage_copies(j, stage):
                c.wait_recv()
            mine = here[order[j][stage]]
            others = [(mine + k) % 4 for k in (1, 2, 3)]
            if stage == 0:
                total = rsb[j, core, pl.ds(mine * 16, 16)].astype(F32)
                for o in others:
                    total = total + r1[j, o].astype(F32)
                r1[j, mine] = total.astype(BF)
            elif stage == 1:
                total = r1[j, here[order[j][0]], pl.ds(mine * 4, 4)].astype(F32)
                for o in others:
                    total = total + r2[j, o].astype(F32)
                r2[j, mine] = total.astype(BF)
            else:
                total = r2[j, here[order[j][1]], mine].astype(F32)
                for o in others:
                    total = total + r3[j, o].astype(F32)
                dw_o[j] = total

        weight_grads(0)
        core_copy(0).start()
        weight_grads(1)
        core_copy(1).start()
        core_sum(0)
        stage_start(0, 0)
        weight_grads(2)
        core_copy(2).start()
        core_sum(1)
        stage_start(1, 0)

        arrived[4]()
        regroup(mix_in, xc)
        core_sum(2)
        stage_start(2, 0)

        def attention_out(i):
            return pltpu.make_async_copy(mix_r.at[i], att_o.at[i], osem.at[i])

        @pl.loop(0, 8)
        def _(i):
            factors = pltpu.roll(coef[...], (128 - i * 8) % 128, 1)
            for h in range(HEADS):
                both = mix_r[i, :, cols(h)].astype(F32) * factors[:, h : h + 1]
                both = both + xc[i, :, cols(h)].astype(F32) * factors[:, 64 + h : 65 + h]
                mix_r[i, :, cols(h)] = both.astype(BF)
            attention_out(i).start()

        stage_sum(0, 0)
        stage_start(0, 1)
        arrived[5]()
        arrived[6]()
        regroup(dx_in, gc)
        stage_sum(1, 0)
        stage_start(1, 1)

        def input_out(t):
            return pltpu.make_async_copy(x_v.at[:, :, half(t)], dx_o.at[:, :, half(t)], osem.at[8 + t])

        for t in range(2):
            whole = input_tile(0, t) + gc[:, :, t * 512 : t * 512 + 512].reshape(1024, 512).astype(F32)
            x_v[:, :, t * 512 : t * 512 + 512] = whole.astype(BF).reshape(8, 128, 512)
            input_out(t).start()
            if t == 0:
                stage_sum(2, 0)
                stage_start(2, 1)
                stage_sum(0, 1)
                stage_start(0, 2)
        stage_sum(1, 1)
        stage_start(1, 2)
        stage_sum(2, 1)
        stage_start(2, 2)
        for j in range(3):
            stage_sum(j, 2)

        for m in moves:
            m[2]()
        for j in range(3):
            core_copy(j).wait_send()
            for stage in range(3):
                for c in stage_copies(j, stage):
                    c.wait_send()
        for i in range(8):
            attention_out(i).wait()
        for t in range(2):
            input_out(t).wait()

    return kernel


def body(tokens, lengths, w_qkv, out_grad):
    tok3 = tokens.reshape(8, 128, 1024)
    g3 = out_grad.reshape(8, 128, 1024)
    tok4 = tok3.reshape(8, 16, 8, 1024)
    g4 = g3.reshape(8, 16, 8, 1024)
    any_spec = pl.BlockSpec(memory_space=pl.ANY)
    vm = pltpu.VMEM
    dma = pltpu.SemaphoreType.DMA
    attention, input_grad, w_grads = pl.pallas_call(
        make_kernel(lax.axis_size("dp"), lax.axis_size("seq")),
        out_shape=(
            jax.ShapeDtypeStruct((8, 128, 1024), BF),
            jax.ShapeDtypeStruct((8, 128, 1024), BF),
            jax.ShapeDtypeStruct((3, 64, 128), F32),
        ),
        in_specs=[pl.BlockSpec(memory_space=pltpu.SMEM)] + [any_spec] * 5,
        out_specs=(any_spec, any_spec, pl.BlockSpec(memory_space=vm)),
        scratch_shapes=[
            vm((8, 128, 1024), BF),
            vm((8, 128, 1024), BF),
            vm((3, 1024, 1024), BF),
            vm((16, 8, 8, 1024), BF),
            vm((16, 8, 8, 1024), BF),
            vm((8, 128, 1024), BF),
            vm((8, 128, 1024), BF),
            vm((3, 16, 128, 1024), BF),
            vm((8, 128, 1024), BF),
            vm((8, 16, 8, 1024), BF),
            vm((16, 8, 8, 1024), BF),
            vm((8, 16, 8, 1024), BF),
            vm((16, 8, 8, 1024), BF),
            vm((1024, 2048), BF),
            vm((3, 2, 64, 64, 128), BF),
            vm((3, 64, 64, 128), BF),
            vm((3, 4, 16, 64, 128), BF),
            vm((3, 4, 4, 64, 128), BF),
            vm((3, 4, 64, 128), BF),
            vm((2, 3, 128, 128), F32),
            vm((2, 16, 3, 8, 128), F32),
            vm((2, 16, 3, 8, 128), F32),
            vm((2, 2, 64, 128), F32),
            vm((128, 128), F32),
            dma((5,)),
            dma((10,)),
            dma((7,)),
            dma((7, 16)),
            dma((7, 16)),
            dma((3,)),
            dma((3,)),
            dma((9, 4)),
            dma((9, 4)),
        ],
        compiler_params=pltpu.CompilerParams(
            collective_id=0, has_side_effects=True, vmem_limit_bytes=67043328
        ),
        name="strided_attention",
    )(lengths, tok3, tok4, g3, g4, w_qkv)
    return (attention.reshape(tokens.shape), input_grad.reshape(tokens.shape), w_grads)


def solution(mesh):
    in_specs = (P("dp", "seq", None, None), P("dp"), P(), P("dp", "seq", None, None))
    out_specs = (P("dp", "seq", None, None), P("dp", "seq", None, None), P(None, "seq", "dp"))
    return jax.shard_map(body, mesh=mesh, in_specs=in_specs, out_specs=out_specs, check_vma=False)
```

```python
import math

import jax
import jax.numpy as jnp
from jax import lax
from jax.experimental import pallas as pl
from jax.experimental.pallas import tpu as pltpu
from jax.sharding import PartitionSpec as P

BF = jnp.bfloat16
F32 = jnp.float32
SCALE = 1.0 / math.sqrt(128.0)
HEADS = 8
NT_W = 512
MESH = pl.DeviceIdType.MESH


def nt(a, b):
    return lax.dot_general(a, b, (((1,), (1,)), ((), ())), preferred_element_type=F32)


def tn(a, b):
    return lax.dot_general(a, b, (((0,), (0,)), ((), ())), preferred_element_type=F32)


def nn(a, b):
    return jnp.dot(a, b, preferred_element_type=F32)


def cols(h):
    return slice(h * 128, h * 128 + 128)


def tile(t, width):
    return pl.ds(pl.multiple_of(t * width, width), width)


def allowed(side, index, length):
    key = lax.broadcasted_iota(jnp.int32, (128, 128), 0)
    query = lax.broadcasted_iota(jnp.int32, (128, 128), 1)
    if side == 0:
        return (key <= query) & ((index * 128 + key < length) | (key == query))
    return (key < query) & (key * 128 + index < length)


def pipelined(blocks, gap, first, second, third):
    count = len(blocks)
    for n in range(count + 2 * gap):
        if n < count:
            first(*blocks[n])
        if 0 <= n - gap < count:
            second(*blocks[n - gap])
        if 0 <= n - 2 * gap < count:
            third(*blocks[n - 2 * gap])


def project(x_ref, w_ref, qkv, j):
    @pl.loop(0, 1024 // NT_W)
    def _(t):
        out = nn(x_ref[...].reshape(1024, 1024), w_ref[j, :, tile(t, NT_W)])
        qkv[j, 0:8, :, tile(t, NT_W)] = out.astype(BF).reshape(8, 128, NT_W)


def project_group(xc, w_ref, qkv, group):
    rows = tile(group, 32)

    @pl.loop(0, 3 * (1024 // NT_W))
    def _(n):
        j, t = n // (1024 // NT_W), n % (1024 // NT_W)
        out = nn(xc[:, rows, :].reshape(256, 1024), w_ref[j, :, tile(t, NT_W)])
        qkv[j, 8:16, rows, tile(t, NT_W)] = out.astype(BF).reshape(8, 32, NT_W)


def row_stats(qkv, g_ref, stats, me, length):
    @pl.loop(0, 8)
    def _(i):
        mask = allowed(0, me * 8 + i, length)
        scores = {}

        def first(h):
            scores[h] = (
                nt(qkv[1, i, :, cols(h)], qkv[0, i, :, cols(h)]),
                nt(qkv[2, i, :, cols(h)], g_ref[i, :, cols(h)]),
            )

        def second(h):
            score, grad = scores.pop(h)
            score = jnp.where(mask, score * SCALE, -1e30)
            highest = jnp.max(score, axis=0, keepdims=True)
            weight = jnp.exp(score - highest)
            row = pl.ds(i * 8 + h, 1)
            stats[0, 0, row, :] = highest
            stats[0, 1, row, :] = jnp.sum(weight, axis=0, keepdims=True)
            stats[0, 2, row, :] = jnp.sum(weight * grad, axis=0, keepdims=True)

        pipelined([(h,) for h in range(HEADS)], 2, first, second, lambda h: None)


def column_forward(qkv, other, stats, joint, mix_c, me, length):
    @pl.loop(0, 8)
    def _(i):
        mask = allowed(1, me * 8 + i, length)
        scores, probs = {}, {}

        def first(h):
            scores[h] = nt(qkv[1, 8 + i, :, cols(h)], qkv[0, 8 + i, :, cols(h)])

        def second(h):
            row = pl.ds(i * 8 + h, 1)
            score = jnp.where(mask, scores.pop(h) * SCALE, -1e30)
            highest = jnp.max(score, axis=0, keepdims=True)
            weight = jnp.exp(score - jnp.maximum(highest, -1e29))
            total = jnp.sum(weight, axis=0, keepdims=True)
            row_highest = other[0, row, :]
            top = jnp.maximum(highest, row_highest)
            own_factor = jnp.exp(highest - top)
            row_factor = jnp.exp(row_highest - top)
            inverse = 1.0 / (total * own_factor + other[1, row, :] * row_factor)
            own_share = own_factor * inverse
            row_share = row_factor * inverse
            stats[1, 0, row, :] = highest
            stats[1, 1, row, :] = row_share
            stats[1, 2, row, :] = other[2, row, :] * row_share
            joint[1, 0, row, :] = own_share
            probs[h] = (weight * own_share).astype(BF)

        def third(h):
            mixed = tn(probs.pop(h), qkv[2, 8 + i, :, cols(h)])
            mix_c[i, :, :, cols(h)] = mixed.reshape(16, 8, 128).astype(BF)

        pipelined([(h,) for h in range(HEADS)], 2, first, second, third)


def attend_back(qkv, g_ref, stats, joint, side, me, length, heads, per_step, mix=None):
    @pl.loop(0, 8 // per_step)
    def _(step):
        index = [step * per_step + n for n in range(per_step)]
        masks = [allowed(side, me * 8 + i, length) for i in index]
        scores, probs = {}, {}

        def first(n, h):
            at = side * 8 + index[n]
            scores[n, h] = (
                nt(qkv[1, at, :, cols(h)], qkv[0, at, :, cols(h)]),
                nt(qkv[2, at, :, cols(h)], g_ref[index[n], :, cols(h)]),
            )

        def second(n, h):
            score, grad = scores.pop((n, h))
            row = pl.ds(index[n] * 8 + h, 1)
            prob = jnp.exp(score * SCALE - stats[side, 0, row, :]) * joint[side, 0, row, :]
            prob = jnp.where(masks[n], prob, 0.0)
            if side == 1:
                delta = stats[1, 2, row, :] + jnp.sum(prob * grad, axis=0, keepdims=True)
                joint[1, 1, row, :] = delta
            else:
                delta = joint[0, 1, row, :]
            probs[n, h] = (prob.astype(BF), (prob * (grad - delta)).astype(BF))

        def third(n, h):
            at = side * 8 + index[n]
            prob, grad_score = probs.pop((n, h))
            grad_value = nn(prob, g_ref[index[n], :, cols(h)])
            if mix is not None:
                mix[index[n], :, cols(h)] = tn(prob, qkv[2, at, :, cols(h)]).astype(BF)
            grad_key = nn(grad_score, qkv[0, at, :, cols(h)]) * SCALE
            grad_query = tn(grad_score, qkv[1, at, :, cols(h)]) * SCALE
            qkv[2, at, :, cols(h)] = grad_value.astype(BF)
            qkv[1, at, :, cols(h)] = grad_key.astype(BF)
            qkv[0, at, :, cols(h)] = grad_query.astype(BF)

        pipelined([(n, h) for n in range(per_step) for h in heads], 2, first, second, third)


def permutation():
    row = lax.broadcasted_iota(jnp.int32, (256, 256), 0)
    col = lax.broadcasted_iota(jnp.int32, (256, 256), 1)
    return ((row // 32 == col % 8) & ((row // 8) % 4 == col // 64) & (row % 8 == (col // 8) % 8)).astype(BF)


def regroup(raw, out, group, lanes):
    width = lanes.stop - lanes.start
    moved = nn(permutation(), raw[pl.ds(group * 4, 4), :, :, lanes].reshape(256, width))
    out[:, tile(group, 32), lanes] = moved.astype(BF).reshape(8, 32, width)


def regroup_add(raw, out, group, lanes):
    width = lanes.stop - lanes.start
    moved = nn(permutation(), raw[pl.ds(group * 4, 4), :, :, lanes].reshape(256, width)).reshape(8, 32, width)
    out[:, tile(group, 32), lanes] = (moved + out[:, tile(group, 32), lanes].astype(F32)).astype(BF)


def transpose_into(x_ref, xt, side):
    @pl.loop(0, 8)
    def _(i):
        xt[:, pl.ds(pl.multiple_of(side * 1024 + i * 128, 128), 128)] = x_ref[i].T


def swap_groups(rows):
    parts = [rows[8 * o : 8 * o + 8, :] for o in range(8)]
    lane = lax.broadcasted_iota(jnp.int32, (8, 128), 1)
    for b in (1, 2, 4):
        high = (lane // b) % 2 == 1
        new = list(parts)
        for v in range(8):
            if v & b == 0:
                new[v] = jnp.where(high, pltpu.roll(parts[v | b], b, 1), parts[v])
                new[v | b] = jnp.where(high, parts[v | b], pltpu.roll(parts[v], 128 - b, 1))
        parts = new
    return jnp.concatenate(parts, axis=0)


def pack(rows, sent, s):
    sent[:, s] = rows.T.reshape(16, 8, 128)


def unpack(came, s):
    return swap_groups(came[:, s].reshape(128, 128).T[:64])


def make_kernel(dp_size, seq_size):
    def kernel(
        len_ref, tok3, tok4, g3, g4, w_hbm, att_o, dx_o, dw_o,
        x_v, g_v, w_v, raw_x, raw_g, xc, gc, qkv, mix_r, mix_c, mix_in, dxs, dx_in, xt,
        rsb, rc, r1, r2, r3, rsb_s, rc_s, r1_s, r2_s, r3_s, stats, sent_r, came_c, sent_c, came_r, other, joint,
        lsem, osem, own_sem, ss, rs, cs, cr, ts, tr,
    ):
        dp = lax.axis_index("dp")
        me = lax.axis_index("seq")
        core = me % 2
        z = (me // 2) % 4
        ylo = me // 8
        x = dp % 4
        yhi = dp // 4
        y = yhi * 2 + ylo
        length = len_ref[0]
        large, small = (rsb, rc, r1, r2, r3), (rsb_s, rc_s, r1_s, r2_s, r3_s)

        def along(axis, k):
            if axis == "x":
                c = (x + k) % 4
                return (yhi * 4 + c, me), c
            if axis == "y":
                c = (y + k) % 4
                return ((c // 2) * 4 + x, (c % 2) * 8 + z * 2 + core), c
            c = (z + k) % 4
            return (dp, ylo * 8 + c * 2 + core), c

        here = {"x": x, "y": y, "z": z}

        loads = [pltpu.make_async_copy(w_hbm.at[j], w_v.at[j], lsem.at[j]) for j in range(3)]
        loads.append(pltpu.make_async_copy(tok3, x_v, lsem.at[3]))
        loads.append(pltpu.make_async_copy(g3, g_v, lsem.at[4]))
        for at in (3, 0, 4, 1, 2):
            loads[at].start()

        barrier = pltpu.get_barrier_semaphore()

        @pl.loop(1, 16)
        def _(k):
            pl.semaphore_signal(barrier, inc=1, device_id=(dp, (me + k) % 16), device_id_type=MESH)

        for k in (1, 2, 3):
            pl.semaphore_signal(barrier, inc=1, device_id=along("x", k)[0], device_id_type=MESH)
        for c in (0, 1):
            pl.semaphore_signal(
                barrier, inc=1, device_id=((1 - yhi) * 4 + x, c * 8 + z * 2 + core), device_id_type=MESH
            )
        pl.semaphore_wait(barrier, 20)

        def partner(dy, dz, dc):
            return ((ylo + dy) % 2) * 8 + ((z + dz) % 4) * 2 + (core + dc) % 2

        def exchange(n, src, dst):
            def copy(dy, dz, dc, slot):
                p = partner(dy, dz, dc)
                q = dy * 8 + dz * 2 + dc
                return pltpu.make_async_remote_copy(
                    src(p), dst(slot), ss.at[n, q], rs.at[n, q], device_id=(dp, p), device_id_type=MESH
                )

            def local():
                return pltpu.make_async_copy(src(me), dst(me), own_sem.at[n])

            def start():
                for dz in (0, 1, 3, 2):

                    @pl.loop(1 if dz == 0 else 0, 4)
                    def _(e):
                        copy(e // 2, dz, e % 2, me).start()

                local().start()

            def arrived_from(dy, dz, dc):
                p = partner(dy, 4 - dz, dc)
                q = dy * 8 + dz * 2 + dc
                pltpu.make_async_remote_copy(
                    src(p), dst(p), ss.at[n, q], rs.at[n, q], device_id=(dp, p), device_id_type=MESH
                ).wait_recv()

            def arrived():
                @pl.loop(1, 16)
                def _(q):
                    arrived_from(q // 8, (q // 2) % 4, q % 2)

                local().wait()

            def sent_all():
                @pl.loop(1, 16)
                def _(q):
                    copy(q // 8, (q // 2) % 4, q % 2, me).wait_send()

            return start, arrived, sent_all, arrived_from, local

        half = lambda t: pl.ds(t * 512, 512)
        lane_half = lambda t: slice(t * 512, t * 512 + 512)
        moves = [
            exchange(0, lambda p: tok4.at[:, p], lambda p: raw_x.at[p]),
            exchange(1, lambda p: sent_r.at[p], lambda p: came_c.at[p]),
            exchange(2, lambda p: g4.at[:, p, :, half(0)], lambda p: raw_g.at[p, :, :, half(0)]),
            exchange(3, lambda p: g4.at[:, p, :, half(1)], lambda p: raw_g.at[p, :, :, half(1)]),
            exchange(4, lambda p: mix_c.at[:, p, :, pl.ds(0, 256)], lambda p: mix_in.at[p, :, :, pl.ds(0, 256)]),
            exchange(5, lambda p: sent_c.at[p], lambda p: came_r.at[p]),
            exchange(6, lambda p: mix_c.at[:, p, :, pl.ds(256, 768)], lambda p: mix_in.at[p, :, :, pl.ds(256, 768)]),
            exchange(7, lambda p: dxs.at[:, p, :, half(0)], lambda p: dx_in.at[p, :, :, half(0)]),
            exchange(8, lambda p: dxs.at[:, p, :, half(1)], lambda p: dx_in.at[p, :, :, half(1)]),
        ]
        start = [m[0] for m in moves]
        arrived = [m[1] for m in moves]

        start[0]()

        loads[3].wait()
        for j in range(3):
            loads[j].wait()
            project(x_v, w_v, qkv, j)
        loads[4].wait()
        stats[...] = jnp.zeros_like(stats)
        row_stats(qkv, g_v, stats, me, length)
        for s in range(3):
            pack(stats[0, s], sent_r, s)
        start[1]()
        start[2]()
        start[3]()
        transpose_into(x_v, xt, 0)

        for n in range(4):
            for dz in (0, 3 - 2 * (z % 2)) if n < 2 else (2, 1 + 2 * (z % 2)):
                for dc in (0, 1):
                    if n == 0 and isinstance(dz, int) and dc == 0:
                        moves[0][4]().wait()
                    else:
                        moves[0][3](n % 2, dz, dc)
            group = ((ylo + n % 2) % 2) * 2 + (z // 2 + n // 2) % 2
            regroup(raw_x, xc, group, slice(0, 1024))
            project_group(xc, w_v, qkv, group)
        arrived[1]()
        for s in range(3):
            other[s] = unpack(came_c, s)
        column_forward(qkv, other, stats, joint, mix_c, me, length)
        start[4]()

        for t in range(2):
            if t == 1:
                transpose_into(xc, xt, 1)
            arrived[2 + t]()

            @pl.loop(0, 4)
            def _(i):
                regroup(raw_g, gc, i, lane_half(t))

            attend_back(qkv, gc, stats, joint, 1, me, length, range(4 * t, 4 * t + 4), 2)
        stats[1, 2, :64, :] = joint[1, 1]
        pack(stats[1, 1], sent_c, 0)
        pack(stats[1, 2], sent_c, 1)
        start[5]()
        start[6]()

        def input_tile(side, t):
            total = None
            for j in range(3):
                grads = qkv[j, side * 8 : side * 8 + 8].reshape(1024, 1024)
                term = nt(grads, w_v[j, tile(t, 512), :])
                total = term if total is None else total + term
            return total

        dxs[:, :, :, lane_half(0)] = input_tile(1, 0).reshape(8, 16, 8, 512).astype(BF)
        start[7]()

        arrived[5]()
        joint[0, 0] = unpack(came_r, 0)
        joint[0, 1] = unpack(came_r, 1)
        attend_back(qkv, g_v, stats, joint, 0, me, length, range(HEADS), 1, mix_r)

        pieces = ((0, 0, 64, "xyz"), (1, 0, 64, "xzy"), (2, 0, 32, "yzx"), (2, 32, 32, "zyx"))

        def buffers(n):
            return [ref.at[n % 2] for ref in (large if n < 2 else small)]

        def weight_grads(j):
            @pl.loop(0, 2)
            def _(t):
                out = nn(xt[...], qkv[j, :, :, tile(t, 512)].reshape(2048, 512)).astype(BF)
                for n, (of, low, rows, order) in enumerate(pieces):
                    if of != j:
                        continue
                    block = buffers(n)[0]
                    for s in range(16):
                        for b in range(4):
                            pos = {"x": b, "y": t * 2 + s // 8, "z": (s // 2) % 4}
                            a1, a2, a3 = (pos[a] for a in order)
                            first = s * 64 + low
                            block[s % 2, a1 * 16 + a2 * 4 + a3] = out[first : first + rows, b * 128 : b * 128 + 128]

        def core_copy(n):
            block, rc = buffers(n)[:2]
            return pltpu.make_async_remote_copy(
                block.at[1 - core], rc, cs.at[n], cr.at[n], device_id=(dp, me + 1 - 2 * core), device_id_type=MESH
            )

        def stage_copies(n, stage):
            order = pieces[n][3]
            block, _, r1, r2, r3 = buffers(n)
            axis = order[stage]
            copies = []
            for k in (1, 2, 3):
                device, c = along(axis, k)
                if stage == 0:
                    src, dst = block.at[core, pl.ds(c * 16, 16)], r1.at[here[axis]]
                elif stage == 1:
                    src, dst = r1.at[here[order[0]], pl.ds(c * 4, 4)], r2.at[here[axis]]
                else:
                    src, dst = r2.at[here[order[1]], c], r3.at[here[axis]]
                at = n * 3 + stage
                copies.append(
                    pltpu.make_async_remote_copy(
                        src, dst, ts.at[at, k], tr.at[at, k], device_id=device, device_id_type=MESH
                    )
                )
            return copies

        def core_sum(n):
            core_copy(n).wait_recv()
            block, rc = buffers(n)[:2]

            @pl.loop(0, 4)
            def _(t):
                at = pl.ds(t * 16, 16)
                block[core, at] = (block[core, at].astype(F32) + rc[at].astype(F32)).astype(BF)

        def stage_start(n, stage):
            for c in stage_copies(n, stage):
                c.start()

        def stage_sum(n, stage):
            for c in stage_copies(n, stage):
                c.wait_recv()
            j, low, rows, order = pieces[n]
            block, _, r1, r2, r3 = buffers(n)
            mine = here[order[stage]]
            if stage == 0:
                total, came = block[core, pl.ds(mine * 16, 16)], r1
            elif stage == 1:
                total, came = r1[here[order[0]], pl.ds(mine * 4, 4)], r2
            else:
                total, came = r2[here[order[1]], mine], r3
            total = total.astype(F32)
            for k in (1, 2, 3):
                total = total + came[(mine + k) % 4].astype(F32)
            if stage < 2:
                came[mine] = total.astype(BF)
            else:
                dw_o[j, low : low + rows] = total

        weight_grads(0)
        core_copy(0).start()
        weight_grads(1)
        core_copy(1).start()
        core_sum(0)
        stage_start(0, 0)
        dxs[:, :, :, lane_half(1)] = input_tile(1, 1).reshape(8, 16, 8, 512).astype(BF)
        start[8]()
        core_sum(1)
        stage_start(1, 0)
        weight_grads(2)
        core_copy(2).start()
        core_copy(3).start()

        arrived[4]()
        arrived[6]()

        def attention_out(i):
            return pltpu.make_async_copy(mix_r.at[:, tile(i, 32)], att_o.at[:, tile(i, 32)], osem.at[i])

        @pl.loop(0, 4)
        def _(i):
            regroup_add(mix_in, mix_r, i, slice(0, 1024))
            attention_out(i).start()

        core_sum(2)
        stage_start(2, 0)
        core_sum(3)
        stage_start(3, 0)

        def input_grads(t):
            x_v[:, :, lane_half(t)] = input_tile(0, t).astype(BF).reshape(8, 128, 512)

        def input_out(t):
            return pltpu.make_async_copy(x_v.at[:, :, half(t)], dx_o.at[:, :, half(t)], osem.at[4 + t])

        def input_sum(t):
            arrived[7 + t]()

            @pl.loop(0, 4)
            def _(i):
                regroup_add(dx_in, x_v, i, lane_half(t))

            input_out(t).start()

        input_grads(0)
        stage_sum(0, 0)
        stage_start(0, 1)
        input_grads(1)
        input_sum(0)
        for n in (1, 2, 3):
            stage_sum(n, 0)
            stage_start(n, 1)
        stage_sum(0, 1)
        stage_start(0, 2)
        input_sum(1)
        for n in (1, 2, 3):
            stage_sum(n, 1)
            stage_start(n, 2)
        for n in range(4):
            stage_sum(n, 2)

        for m in moves:
            m[2]()
        for n in range(4):
            core_copy(n).wait_send()
            for stage in range(3):
                for c in stage_copies(n, stage):
                    c.wait_send()
        for i in range(4):
            attention_out(i).wait()
        for t in range(2):
            input_out(t).wait()

    return kernel


def body(tokens, lengths, w_qkv, out_grad):
    tok3 = tokens.reshape(8, 128, 1024)
    g3 = out_grad.reshape(8, 128, 1024)
    tok4 = tok3.reshape(8, 16, 8, 1024)
    g4 = g3.reshape(8, 16, 8, 1024)
    any_spec = pl.BlockSpec(memory_space=pl.ANY)
    vm = pltpu.VMEM
    dma = pltpu.SemaphoreType.DMA
    attention, input_grad, w_grads = pl.pallas_call(
        make_kernel(lax.axis_size("dp"), lax.axis_size("seq")),
        out_shape=(
            jax.ShapeDtypeStruct((8, 128, 1024), BF),
            jax.ShapeDtypeStruct((8, 128, 1024), BF),
            jax.ShapeDtypeStruct((3, 64, 128), F32),
        ),
        in_specs=[pl.BlockSpec(memory_space=pltpu.SMEM)] + [any_spec] * 5,
        out_specs=(any_spec, any_spec, pl.BlockSpec(memory_space=vm)),
        scratch_shapes=[
            vm((8, 128, 1024), BF),
            vm((8, 128, 1024), BF),
            vm((3, 1024, 1024), BF),
            vm((16, 8, 8, 1024), BF),
            vm((16, 8, 8, 1024), BF),
            vm((8, 128, 1024), BF),
            vm((8, 128, 1024), BF),
            vm((3, 16, 128, 1024), BF),
            vm((8, 128, 1024), BF),
            vm((8, 16, 8, 1024), BF),
            vm((16, 8, 8, 1024), BF),
            vm((8, 16, 8, 1024), BF),
            vm((16, 8, 8, 1024), BF),
            vm((1024, 2048), BF),
            vm((2, 2, 64, 64, 128), BF),
            vm((2, 64, 64, 128), BF),
            vm((2, 4, 16, 64, 128), BF),
            vm((2, 4, 4, 64, 128), BF),
            vm((2, 4, 64, 128), BF),
            vm((2, 2, 64, 32, 128), BF),
            vm((2, 64, 32, 128), BF),
            vm((2, 4, 16, 32, 128), BF),
            vm((2, 4, 4, 32, 128), BF),
            vm((2, 4, 32, 128), BF),
            vm((2, 3, 128, 128), F32),
            vm((16, 3, 8, 128), F32),
            vm((16, 3, 8, 128), F32),
            vm((16, 2, 8, 128), F32),
            vm((16, 2, 8, 128), F32),
            vm((3, 64, 128), F32),
            vm((2, 2, 64, 128), F32),
            dma((5,)),
            dma((6,)),
            dma((9,)),
            dma((9, 16)),
            dma((9, 16)),
            dma((4,)),
            dma((4,)),
            dma((12, 4)),
            dma((12, 4)),
        ],
        compiler_params=pltpu.CompilerParams(
            collective_id=0, has_side_effects=True, vmem_limit_bytes=67043328
        ),
        name="strided_attention",
    )(lengths, tok3, tok4, g3, g4, w_qkv)
    return (attention.reshape(tokens.shape), input_grad.reshape(tokens.shape), w_grads)


def solution(mesh):
    in_specs = (P("dp", "seq", None, None), P("dp"), P(), P("dp", "seq", None, None))
    out_specs = (P("dp", "seq", None, None), P("dp", "seq", None, None), P(None, "seq", "dp"))
    return jax.shard_map(body, mesh=mesh, in_specs=in_specs, out_specs=out_specs, check_vma=False)
```
